32 devices in a mesh: seq: 16 (over z, x, core), group: 2 (over y).
Axes of the slice: x: 2, y: 2, z: 4, core: 2. Of those that a mesh axis runs over, the one named last changes fastest.
Arguments:
- prefix_keys: bfloat16 [4096, 512], P(('group', 'seq')), parts along dimension 0, may hold values from -5 to 5
- prefix_values: bfloat16 [4096, 512], P(('group', 'seq')), parts along dimension 0, may hold values from -6 to 6
- round_queries: bfloat16 [2048, 2048], P(('group', 'seq')), parts along dimension 0, may hold values from -5 to 5
- round_keys: bfloat16 [2048, 512], P(('group', 'seq')), parts along dimension 0, may hold values from -5 to 5
- round_values: bfloat16 [2048, 512], P(('group', 'seq')), parts along dimension 0, may hold values from -6 to 6
- d_out: bfloat16 [2048, 2048], P(('group', 'seq')), parts along dimension 0, may hold values from -6 to 6
- prefix_agent: int32 [4096], P('group'), parts along dimension 0, may hold values from 0 to 7
- prefix_round: int32 [4096], P('group'), parts along dimension 0, may hold values from 0 to 15, never falling along the last dimension, each value on 1 to 256 neighbouring positions
- round_agent: int32 [2048], P('group'), parts along dimension 0, may hold values from 0 to 7
Outputs:
- attn_out: bfloat16 [2048, 2048], P(('group', 'seq')), parts along dimension 0
- d_round_queries: bfloat16 [2048, 2048], P(('group', 'seq')), parts along dimension 0
- d_round_keys: bfloat16 [2048, 512], P(('group', 'seq')), parts along dimension 0
- d_round_values: bfloat16 [2048, 512], P(('group', 'seq')), parts along dimension 0
- d_prefix_keys: bfloat16 [4096, 512], P(('group', 'seq')), parts along dimension 0
- d_prefix_values: bfloat16 [4096, 512], P(('group', 'seq')), parts along dimension 0
The draws below stay inside these ranges and needn't reach their ends.
There are 2 independent parts, one for each index of `group`. The reference program is written for one: setup_inputs(seed, part) draws one part's arguments, and reference() takes and returns one part's arrays. A program takes and returns all parts, laid end to end along the dimension named above; each array names one. Nothing has to cross between parts.
Inputs may be any that keep to these rules, and one draw needn't show every extreme that they name: `prefix_round`: never falls along positions; every round has at least one token.
All inputs are finite; a program needn't handle non-finite values.
Results may differ from the reference program's by a relative error of at most 0.017.
Values may be sent and summed in bfloat16 or wider, within the bound.
A program may use at most 128 MiB of HBM per device.

```python
import math
import jax
import jax.numpy as jnp
import numpy as np

HQ = 16
KVH = 4
DH = 128
AGENTS = 8
ROUNDS = 16
ROUND = 1024
PRE = 2048
GRP = 4


def draw_round_queries(key, part):
    sample = jax.random.normal(jax.random.fold_in(key, 11), (ROUND, HQ * DH), jnp.float32)
    values = jnp.clip(sample, -5.0, 5.0)
    return values.astype(jnp.bfloat16)


def draw_round_keys(key, part):
    sample = jax.random.normal(jax.random.fold_in(key, 21), (ROUND, KVH * DH), jnp.float32)
    values = jnp.clip(sample, -5.0, 5.0)
    return values.astype(jnp.bfloat16)


def plant(values, rng, low, largest):
    spot = [jax.random.randint(jax.random.fold_in(rng, axis), (), 0, length) for axis, length in enumerate(values.shape)]
    longest = values.shape.index(max(values.shape))
    beside = spot[:longest] + [(spot[longest] + 1) % values.shape[longest]] + spot[longest + 1:]
    return values.at[tuple(spot)].set(low).at[tuple(beside)].set(largest)


def block_levels(rng, extent, split, least, top_value):
    level = 1.0
    for dim, parts in split:
        heights = jax.random.uniform(jax.random.fold_in(jax.random.fold_in(rng, 6), dim), (parts,), jnp.float32, least / len(split), top_value / len(split))
        level = level * jnp.repeat(jnp.exp(heights), extent[dim] // parts).reshape((-1,) + (1,) * (len(extent) - 1 - dim))
    return level


def split_up(amount, total, most, lean):
    weights = [(1 << 20) // math.isqrt(grade ** lean) + 1 for grade in range(2, amount + 1)]
    rest, holding = total - most - (amount - 1), [1] * (amount - 1)
    while rest > 0:
        free = [i for i in range(amount - 1) if holding[i] < most]
        mass, remaining = sum([weights[i] for i in free]), rest
        for i in free:
            more = min(most - holding[i], max(1, remaining * weights[i] // mass), rest)
            holding[i] = holding[i] + more
            rest = rest - more
    return np.array([most] + holding)


def ragged(stream_key, count, total, most, lean):
    if count == 2:
        one = jax.random.randint(stream_key, (), max(1, total - most), min(most, total - 1) + 1)
        return jnp.stack([one, total - one])
    tallies = jnp.asarray(split_up(count, total, most, lean), jnp.int32)
    pairs = (count - 1) // 2
    donor, taker = tallies[1:1 + 2 * pairs:2], tallies[2:2 + 2 * pairs:2]
    slack = jnp.minimum(donor - 1, most - taker)
    passed = jax.random.randint(jax.random.fold_in(stream_key, 1), (pairs,), 0, 1 << 20) % (slack + 1)
    tallies = tallies.at[1:1 + 2 * pairs:2].set(donor - passed).at[2:2 + 2 * pairs:2].set(taker + passed)
    return tallies[jax.random.permutation(jax.random.fold_in(stream_key, 2), count)]


def gaussian(own_key, dims, spread, limit, pieces=(), held_as=jnp.bfloat16):
    level = block_levels(own_key, dims, pieces, -0.22, 0.18) if pieces else 1.0
    drawn = jax.random.normal(own_key, dims, jnp.float32) * spread * level
    return jnp.minimum(jnp.maximum(drawn, -limit), limit).astype(held_as)


def setup_inputs(seed: int = 0, part: int = 0) -> dict:
    arg_keys = jax.random.split(jax.random.key(seed), 10)
    part_splits = jax.random.split(jax.random.fold_in(arg_keys[9], part), 10)
    return {
        "prefix_keys": gaussian(part_splits[0], (PRE, KVH * DH), 1.0, 5.0, ((0, 16),)),
        "prefix_values": gaussian(part_splits[1], (PRE, KVH * DH), 1.0, 6.0, ((0, 16),)),
        "round_queries": draw_round_queries(jax.random.fold_in(jax.random.fold_in(arg_keys[9], part), 71), part),
        "round_keys": draw_round_keys(jax.random.fold_in(jax.random.fold_in(arg_keys[9], part), 71), part),
        "round_values": gaussian(part_splits[4], (ROUND, KVH * DH), 1.0, 6.0, ((0, 16),)),
        "d_out": gaussian(part_splits[5], (ROUND, HQ * DH), 1.0, 6.0, ((0, 16),)),
        "prefix_agent": plant(jax.random.randint(part_splits[6], (PRE,), 0, AGENTS), jax.random.fold_in(part_splits[6], 1), 0, AGENTS - 1).astype(jnp.int32),
        "prefix_round": jnp.searchsorted(jnp.cumsum(ragged(part_splits[7], ROUNDS, PRE, PRE // 8, 2)), jnp.arange(PRE), side="right").astype(jnp.int32),
        "round_agent": plant(jax.random.randint(part_splits[8], (ROUND,), 0, AGENTS), jax.random.fold_in(part_splits[8], 1), 0, AGENTS - 1).astype(jnp.int32),
    }


def reference(prefix_keys, prefix_values, round_queries, round_keys, round_values, d_out, prefix_agent, prefix_round, round_agent):
    score_scale = DH ** -0.5
    keys = jnp.concatenate([prefix_keys, round_keys], 0)
    values = jnp.concatenate([prefix_values, round_values], 0)
    public = prefix_round < ROUNDS - 2
    seen_prefix = public[None, :] | (prefix_agent[None, :] == round_agent[:, None])
    order = jnp.arange(ROUND, dtype=jnp.int32)
    seen_round = order[None, :] <= order[:, None]
    seen = jnp.concatenate([seen_prefix, seen_round], 1)
    outputs = []
    query_grads = []
    key_grads = []
    value_grads = []
    for kv_index in range(KVH):
        key_head = keys[:, kv_index * DH:(kv_index + 1) * DH]
        value_head = values[:, kv_index * DH:(kv_index + 1) * DH]
        key_acc = jnp.zeros((PRE + ROUND, DH), jnp.float32)
        value_acc = jnp.zeros((PRE + ROUND, DH), jnp.float32)
        for inner in range(GRP):
            head_index = kv_index * GRP + inner
            query = round_queries[:, head_index * DH:(head_index + 1) * DH]
            cotangent = d_out[:, head_index * DH:(head_index + 1) * DH]
            raw = jnp.dot(query, key_head.T, preferred_element_type=jnp.float32) * score_scale
            masked = jnp.where(seen, raw, -jnp.inf)
            top_score = jnp.max(masked, 1, keepdims=True)
            log_total = top_score + jnp.log(jnp.sum(jnp.exp(masked - top_score), 1, keepdims=True))
            probs = jnp.exp(masked - log_total)
            probs_low = probs.astype(jnp.bfloat16)
            attended = jnp.dot(probs_low, value_head, preferred_element_type=jnp.float32).astype(jnp.bfloat16)
            outputs.append(attended)
            delta = jnp.sum(cotangent.astype(jnp.float32) * attended.astype(jnp.float32), 1, keepdims=True)
            grad_probs = jnp.dot(cotangent, value_head.T, preferred_element_type=jnp.float32)
            grad_scores = (probs * (grad_probs - delta) * score_scale).astype(jnp.bfloat16)
            query_grads.append(jnp.dot(grad_scores, key_head, preferred_element_type=jnp.float32).astype(jnp.bfloat16))
            key_acc = key_acc + jnp.dot(grad_scores.T, query, preferred_element_type=jnp.float32)
            value_acc = value_acc + jnp.dot(probs_low.T, cotangent, preferred_element_type=jnp.float32)
        key_grads.append(key_acc.astype(jnp.bfloat16))
        value_grads.append(value_acc.astype(jnp.bfloat16))
    attn_out = jnp.concatenate(outputs, 1)
    d_round_queries = jnp.concatenate(query_grads, 1)
    grad_keys = jnp.concatenate(key_grads, 1)
    grad_values = jnp.concatenate(value_grads, 1)
    return (attn_out, d_round_queries, grad_keys[PRE:], grad_values[PRE:], grad_keys[:PRE], grad_values[:PRE])
```

```python
import functools
import math

import jax
import jax.numpy as jnp
from jax import lax
from jax.experimental import pallas as pl
from jax.experimental.pallas import tpu as pltpu
from jax.sharding import PartitionSpec as P

HQ = 16
KVH = 4
DH = 128
ROUNDS = 16


def to_head_rows(local, devices):
    splits = devices // HQ
    quarter_rows = local.shape[0] // splits
    shaped = local.reshape(splits, quarter_rows, HQ, DH).transpose(2, 0, 1, 3)
    return shaped.reshape(devices, quarter_rows, DH)


def from_head_rows(received, devices):
    splits = devices // HQ
    quarter_rows = received.shape[1]
    shaped = received.reshape(HQ, splits, quarter_rows, DH).transpose(1, 2, 0, 3)
    return shaped.reshape(splits * quarter_rows, HQ * DH)


def spread_heads(local, devices):
    local_keys = local.shape[0]
    shaped = local.reshape(local_keys, KVH, DH).transpose(1, 0, 2)
    shaped = jnp.broadcast_to(shaped[:, None], (KVH, devices // KVH, local_keys, DH))
    return shaped.reshape(devices, local_keys, DH)


def sum_groups(received, devices):
    local_keys = received.shape[1]
    summed = received.reshape(KVH, devices // KVH, local_keys, DH).sum(1)
    return summed.transpose(1, 0, 2).reshape(local_keys, KVH * DH)


def body(
    prefix_keys,
    prefix_values,
    round_queries,
    round_keys,
    round_values,
    d_out,
    prefix_agent,
    prefix_round,
    round_agent,
):
    devices = lax.axis_size("seq")
    device_index = lax.axis_index("seq")
    splits = devices // HQ
    own_rows = round_queries.shape[0]
    quarter_rows = own_rows // splits
    pre_rows = prefix_keys.shape[0]
    local_keys = pre_rows + own_rows
    score_scale = DH ** (-0.5)
    own_block = device_index % splits
    keys_local = jnp.concatenate([prefix_keys, round_keys], 0)
    values_local = jnp.concatenate([prefix_values, round_values], 0)
    query_head, grad_head = (
        lax.all_to_all(
            to_head_rows(round_queries, devices), "seq", split_axis=0, concat_axis=0, tiled=True
        ),
        lax.all_to_all(
            to_head_rows(d_out, devices), "seq", split_axis=0, concat_axis=0, tiled=True
        ),
    )
    query_head = query_head.reshape(devices * quarter_rows, DH)
    grad_head = grad_head.reshape(devices * quarter_rows, DH)
    head_rows = devices * quarter_rows
    key_head, value_head = (
        lax.all_to_all(
            spread_heads(keys_local, devices), "seq", split_axis=0, concat_axis=0, tiled=True
        ),
        lax.all_to_all(
            spread_heads(values_local, devices), "seq", split_axis=0, concat_axis=0, tiled=True
        ),
    )
    source = jnp.arange(devices, dtype=jnp.int32)
    query_pos = (
        source[:, None] * own_rows
        + own_block * quarter_rows
        + jnp.arange(quarter_rows, dtype=jnp.int32)[None, :]
    ).reshape(-1)
    query_agent = round_agent[query_pos]
    key_slot = jnp.arange(local_keys, dtype=jnp.int32)
    pre_index = source[:, None] * pre_rows + jnp.minimum(key_slot, pre_rows - 1)[None, :]
    round_index = source[:, None] * own_rows + jnp.maximum(key_slot - pre_rows, 0)[None, :]
    key_agent = prefix_agent[pre_index]
    key_public = prefix_round[pre_index] < ROUNDS - 2
    key_prefix = jnp.broadcast_to((key_slot < pre_rows)[None, :], (devices, local_keys))
    block_shards = math.gcd(devices, 16)
    blocks = devices // block_shards
    block_keys = block_shards * local_keys
    key_blocks = key_head.reshape(blocks, block_keys, DH)
    value_blocks = value_head.reshape(blocks, block_keys, DH)
    key_info = (
        key_agent.reshape(blocks, block_keys),
        key_public.reshape(blocks, block_keys),
        key_prefix.reshape(blocks, block_keys),
        round_index.reshape(blocks, block_keys),
    )

    def block_scores(key_blk, info):
        agent_b, public_b, prefix_b, order_b = info
        visible = jnp.where(
            prefix_b[None, :],
            public_b[None, :] | (agent_b[None, :] == query_agent[:, None]),
            order_b[None, :] <= query_pos[:, None],
        )
        raw = (
            jnp.einsum("qd,kd->qk", query_head, key_blk, preferred_element_type=jnp.float32)
            * score_scale
        )
        return jnp.where(visible, raw, -jnp.inf)

    def stat_step(carry, blk):
        top, total = carry
        masked = block_scores(blk[0], blk[1])
        new_top = jnp.maximum(top, jnp.max(masked, 1, keepdims=True))
        total = total * jnp.exp(top - new_top) + jnp.sum(
            jnp.exp(masked - new_top), 1, keepdims=True
        )
        return ((new_top, total), None)

    start_stats = (
        jnp.full((head_rows, 1), -1e30, jnp.float32),
        jnp.zeros((head_rows, 1), jnp.float32),
    )
    (top_score, total_exp), _ = lax.scan(stat_step, start_stats, (key_blocks, key_info))
    log_total = top_score + jnp.log(total_exp)

    def out_step(acc, blk):
        masked = block_scores(blk[0], blk[2])
        probs_low = jnp.exp(masked - log_total).astype(jnp.bfloat16)
        return (acc + jnp.dot(probs_low, blk[1], preferred_element_type=jnp.float32), None)

    out_acc, _ = lax.scan(
        out_step, jnp.zeros((head_rows, DH), jnp.float32), (key_blocks, value_blocks, key_info)
    )
    attended = out_acc.astype(jnp.bfloat16)
    attn_rows = lax.all_to_all(
        attended.reshape(devices, quarter_rows, DH), "seq", split_axis=0, concat_axis=0, tiled=True
    )
    attn_out = from_head_rows(attn_rows, devices)
    delta = jnp.sum(grad_head.astype(jnp.float32) * attended.astype(jnp.float32), 1, keepdims=True)

    def back_step(acc, blk):
        key_blk, value_blk, info = blk
        masked = block_scores(key_blk, info)
        probs = jnp.exp(masked - log_total)
        grad_probs = jnp.einsum(
            "qd,kd->qk", grad_head, value_blk, preferred_element_type=jnp.float32
        )
        grad_scores = (probs * (grad_probs - delta) * score_scale).astype(jnp.bfloat16)
        acc = acc + jnp.dot(grad_scores, key_blk, preferred_element_type=jnp.float32)
        key_part = jnp.einsum(
            "qk,qd->kd", grad_scores, query_head, preferred_element_type=jnp.float32
        )
        value_part = jnp.einsum(
            "qk,qd->kd", probs.astype(jnp.bfloat16), grad_head, preferred_element_type=jnp.float32
        )
        return (acc, (key_part, value_part))

    start_grad = jnp.zeros((head_rows, DH), jnp.float32)
    query_acc, parts = lax.scan(
        lambda acc, blk: back_step(acc, blk), start_grad, (key_blocks, value_blocks, key_info)
    )
    key_part = parts[0].reshape(devices, local_keys, DH)
    value_part = parts[1].reshape(devices, local_keys, DH)
    key_sum, value_sum = (
        lax.all_to_all(key_part, "seq", split_axis=0, concat_axis=0, tiled=True),
        lax.all_to_all(value_part, "seq", split_axis=0, concat_axis=0, tiled=True),
    )
    grad_keys = sum_groups(key_sum, devices)
    grad_values = sum_groups(value_sum, devices)
    grad_query = query_acc.astype(jnp.bfloat16)
    query_rows = lax.all_to_all(
        grad_query.reshape(devices, quarter_rows, DH),
        "seq",
        split_axis=0,
        concat_axis=0,
        tiled=True,
    )
    d_round_queries = from_head_rows(query_rows, devices)
    keys_low = grad_keys.astype(jnp.bfloat16)
    values_low = grad_values.astype(jnp.bfloat16)
    return (
        attn_out,
        d_round_queries,
        keys_low[pre_rows:],
        values_low[pre_rows:],
        keys_low[:pre_rows],
        values_low[:pre_rows],
    )


MESH = pl.DeviceIdType.MESH
LANES = 4
BIG = 32768.0
F32 = jnp.float32
BF16 = jnp.bfloat16


def mm(a, b):
    return jnp.dot(a, b, preferred_element_type=F32)


def plane_kernel(
    pre, own,
    pk_ref, pv_ref, q_ref, rk_ref, rv_ref, do_ref, pa_ref, pr_ref, ra_ref,
    attn_ref, dq_ref, dk_ref, dv_ref,
    kv_stage, q_stage, kv_buf, q_buf, kext, tri, qt, dot_t, qs, dos,
    s_buf, p_buf, ds_buf, mx_ref, l_ref, acc_t, kt_buf, vt_buf,
    att_stage, dq_stage, red_stage, red_buf, own_part, fin_stage,
    kvz_s, kvz_r, qz_s, qz_r, pg_s, pg_r, red_s, red_r,
    at_s, at_r, dqs_s, dqs_r, fk_s, fk_r, fv_s, fv_r,
):
    keys = pre + own
    rows = LANES * own
    span = LANES * keys
    me = lax.axis_index("seq")
    z = me // LANES
    p = me % LANES
    seq = lambda zz, pp: {"seq": zz * LANES + pp}
    z_peers = [(z + k) % LANES for k in (2, 3, 1)]
    pair = p + 1 - 2 * (p % 2)
    far = (p + 2) % LANES
    cross = pair + 2 - 4 * (pair // 2)
    p_peers = [cross, far, pair]
    scale = DH ** (-0.5)
    to_two = scale * math.log2(math.e)

    def rcopy(src, dst, ss, rs, zz, pp):
        return pltpu.make_async_remote_copy(
            src_ref=src, dst_ref=dst, send_sem=ss, recv_sem=rs,
            device_id=seq(zz, pp), device_id_type=MESH,
        )

    barrier = pltpu.get_barrier_semaphore()
    for o in z_peers:
        pl.semaphore_signal(barrier, inc=1, device_id=seq(o, p), device_id_type=MESH)
    for o in p_peers:
        pl.semaphore_signal(barrier, inc=1, device_id=seq(z, o), device_id_type=MESH)

    for g in range(KVH):
        cols = slice(g * DH, (g + 1) * DH)
        kv_stage[g, 0:pre, :] = pk_ref[:, cols]
        kv_stage[g, pre:keys, :] = rk_ref[:, cols]
        kv_stage[g, keys:keys + pre, :] = pv_ref[:, cols]
        kv_stage[g, keys + pre:2 * keys, :] = rv_ref[:, cols]
        wide = slice(g * 4 * DH, (g + 1) * 4 * DH)
        q_stage[g, 0:own, :] = q_ref[:, wide]
        q_stage[g, own:2 * own, :] = do_ref[:, wide]
    pl.semaphore_wait(barrier, 6)

    def kv_send(o):
        return rcopy(kv_stage.at[o], kv_buf.at[p, z], kvz_s.at[o], kvz_r.at[z], o, p)

    def kv_recv(o):
        return rcopy(kv_stage.at[o], kv_buf.at[p, o], kvz_s.at[o], kvz_r.at[o], o, p)

    def q_send(o):
        return rcopy(q_stage.at[o], q_buf.at[z], qz_s.at[o], qz_r.at[z], o, p)

    def q_recv(o):
        return rcopy(q_stage.at[o], q_buf.at[o], qz_s.at[o], qz_r.at[o], o, p)

    def pg_send(o, piece):
        return rcopy(
            kv_buf.at[p, piece], kv_buf.at[p, piece],
            pg_s.at[o, piece], pg_r.at[p, piece], z, o,
        )

    def pg_recv(o, piece):
        return rcopy(
            kv_buf.at[o, piece], kv_buf.at[o, piece],
            pg_s.at[o, piece], pg_r.at[o, piece], z, o,
        )

    for o in z_peers:
        kv_send(o).start()
    kv_buf[p, z] = kv_stage[z]
    q_buf[z] = q_stage[z]
    for o in p_peers:
        pg_send(o, z).start()
    for o in z_peers:
        q_send(o).start()

    lane = lax.broadcasted_iota(jnp.int32, (own, DH), 1) - 16
    sub = lax.broadcasted_iota(jnp.int32, (DH, pre), 0)

    def ext_step(b, carry):
        at = pl.ds(pl.multiple_of(b * pre, pre), pre)
        c = b % LANES
        zz = b // LANES
        base = zz * keys
        off = (pr_ref[:, at] >= ROUNDS - 2) & (pa_ref[:, at] != sub) & (sub < 8)
        kext[c, pl.ds(pl.multiple_of(base, 64), pre), :] = (
            jnp.where(off, 1.0, 0.0).astype(F32).T.astype(BF16)
        )
        late = (lane >= 0) & (lane < b)
        kext[c, pl.ds(pl.multiple_of(base + pre, 64), own), :] = (
            jnp.where(late, 1.0, 0.0).astype(F32).astype(BF16)
        )
        return carry

    lax.fori_loop(0, LANES * LANES, ext_step, 0)
    sub_q = lax.broadcasted_iota(jnp.int32, (DH, rows), 0)
    block_q = (lax.broadcasted_iota(jnp.int32, (DH, rows), 1) // own) * LANES + p
    ext_q = jnp.where(
        ((sub_q < 8) & (sub_q == ra_ref[pl.ds(p, 1), :])) | (sub_q - 16 == block_q), -BIG, 0.0
    ).astype(F32).astype(BF16)
    for h in range(4):
        qt[DH:2 * DH, h * rows:(h + 1) * rows] = ext_q
    row_k = lax.broadcasted_iota(jnp.int32, (span, rows), 0)
    row_q = lax.broadcasted_iota(jnp.int32, (span, rows), 1)
    tri[...] = jnp.where(
        (row_k // keys == row_q // own) & (row_k % keys >= pre)
        & (row_k % keys - pre > row_q % own),
        -BIG, 0.0,
    ).astype(F32)
    mx_ref[...] = jnp.full(mx_ref.shape, -3.0e38, F32)

    for o in z_peers:
        kv_recv(o).wait_recv()
        for d in p_peers:
            pg_send(d, o).start()
    for o in z_peers:
        q_recv(o).wait_recv()
    for h in range(4):
        cols = slice(h * DH, (h + 1) * DH)
        qh = q_buf[:, 0:own, cols].reshape(rows, DH)
        dh = q_buf[:, own:2 * own, cols].reshape(rows, DH)
        qs[h * rows:(h + 1) * rows, :] = qh
        dos[h * rows:(h + 1) * rows, :] = dh
        qt[0:DH, h * rows:(h + 1) * rows] = qh.T
        dot_t[:, h * rows:(h + 1) * rows] = dh.T

    def head_at(h):
        return pl.ds(pl.multiple_of(h * rows, rows), rows)

    def score_chunk(c, diagonal):
        kc = kv_buf[c, :, 0:keys, :].reshape(span, DH)
        vc = kv_buf[c, :, keys:2 * keys, :].reshape(span, DH)
        kt_buf[c] = kc.T
        vt_buf[c] = vc.T

        def step(h, carry):
            full = jnp.concatenate(
                [kv_buf[c, :, 0:keys, :].reshape(span, DH), kext[c]], 1
            )
            s = mm(full, qt[:, head_at(h)])
            if diagonal:
                s = s + tri[...]
            s_buf[c, :, head_at(h)] = s
            mx_ref[:, head_at(h)] = jnp.maximum(
                mx_ref[:, head_at(h)], jnp.max(s, 0, keepdims=True)
            )
            return carry

        lax.fori_loop(0, 4, step, 0)

    score_chunk(p, True)
    for o in (pair, far, cross):
        for piece in [z] + z_peers:
            pg_recv(o, piece).wait_recv()
        score_chunk(o, False)

    def exp_step(h, carry):
        at = head_at(h)
        top = mx_ref[:, at] * to_two
        total = jnp.zeros((1, rows), F32)
        acc = jnp.zeros((DH, rows), F32)
        for c in range(LANES):
            pu = jnp.exp2(s_buf[c, :, at] * to_two - top)
            total = total + jnp.sum(pu, 0, keepdims=True)
            low = pu.astype(BF16)
            p_buf[c, :, at] = low
            acc = acc + mm(vt_buf[c], low)
        inv = 1.0 / total
        out = (acc * inv).astype(BF16)
        outf = out.astype(F32)
        delta = jnp.sum(outf * dot_t[:, at].astype(F32), 0, keepdims=True)
        mx_ref[:, at] = delta
        l_ref[:, at] = inv
        acc_t[:, at] = outf
        return carry

    lax.fori_loop(0, 4, exp_step, 0)
    for h in range(4):
        cols = slice(h * DH, (h + 1) * DH)
        at = slice(h * rows, (h + 1) * rows)
        att_stage[:, :, cols] = acc_t[:, at].T.astype(BF16).reshape(LANES, own, DH)
        dnorm = (dot_t[:, at].astype(F32) * l_ref[:, at]).T
        dos[at, :] = dnorm.astype(BF16)
    wide_z = pl.ds(pl.multiple_of(z * 4 * DH, 4 * DH), 4 * DH)
    one_z = pl.ds(pl.multiple_of(z * DH, DH), DH)

    def at_send(o):
        return rcopy(att_stage.at[o], attn_ref.at[:, wide_z], at_s.at[o], at_r.at[z], o, p)

    def wide_of(o):
        return pl.ds(pl.multiple_of(o * 4 * DH, 4 * DH), 4 * DH)

    def one_of(o):
        return pl.ds(pl.multiple_of(o * DH, DH), DH)

    def at_recv(o):
        return rcopy(att_stage.at[o], attn_ref.at[:, wide_of(o)], at_s.at[o], at_r.at[o], o, p)

    for o in z_peers:
        at_send(o).start()
    attn_ref[:, wide_z] = att_stage[z]
    acc_t[...] = jnp.zeros(acc_t.shape, F32)

    def back_chunk(c):
        def step(h, carry):
            at = head_at(h)
            vc = kv_buf[c, :, keys:2 * keys, :].reshape(span, DH)
            dp = mm(vc, dot_t[:, at])
            pu = p_buf[c, :, at].astype(F32)
            ds = (pu * ((dp - mx_ref[:, at]) * (l_ref[:, at] * scale))).astype(BF16)
            ds_buf[:, at] = ds
            acc_t[:, at] += mm(kt_buf[c], ds)
            return carry

        lax.fori_loop(0, 4, step, 0)
        return mm(ds_buf[...], qs[...]), mm(p_buf[c], dos[...])

    def red_send(o):
        return rcopy(red_stage.at[o], red_buf.at[p], red_s.at[o], red_r.at[p], z, o)

    def red_recv(o):
        return rcopy(red_stage.at[o], red_buf.at[o], red_s.at[o], red_r.at[o], z, o)

    for o in p_peers:
        dkc, dvc = back_chunk(o)
        red_stage[o, :, 0:keys, :] = dkc.astype(BF16).reshape(LANES, keys, DH)
        red_stage[o, :, keys:2 * keys, :] = dvc.astype(BF16).reshape(LANES, keys, DH)
        red_send(o).start()
    dkc, dvc = back_chunk(p)
    own_part[:, 0:keys, :] = dkc.reshape(LANES, keys, DH)
    own_part[:, keys:2 * keys, :] = dvc.reshape(LANES, keys, DH)
    for h in range(4):
        cols = slice(h * DH, (h + 1) * DH)
        at = slice(h * rows, (h + 1) * rows)
        dq_stage[:, :, cols] = acc_t[:, at].T.astype(BF16).reshape(LANES, own, DH)

    def dq_send(o):
        return rcopy(dq_stage.at[o], dq_ref.at[:, wide_z], dqs_s.at[o], dqs_r.at[z], o, p)

    def dq_recv(o):
        return rcopy(dq_stage.at[o], dq_ref.at[:, wide_of(o)], dqs_s.at[o], dqs_r.at[o], o, p)

    for o in z_peers:
        dq_send(o).start()
    dq_ref[:, wide_z] = dq_stage[z]

    for o in (pair, cross, far):
        red_recv(o).wait_recv()
    total = own_part[...]
    for o in p_peers:
        total = total + red_buf[o].astype(F32)
    fin_stage[...] = total.astype(BF16)

    def fk(o, at, r):
        return rcopy(fin_stage.at[o, pl.ds(0, keys)], dk_ref.at[:, at], fk_s.at[o], fk_r.at[r], o, p)

    def fv(o, at, r):
        return rcopy(
            fin_stage.at[o, pl.ds(keys, keys)], dv_ref.at[:, at], fv_s.at[o], fv_r.at[r], o, p
        )

    for o in z_peers:
        fk(o, one_z, z).start()
        fv(o, one_z, z).start()
    dk_ref[:, one_z] = fin_stage[z, 0:keys, :]
    dv_ref[:, one_z] = fin_stage[z, keys:2 * keys, :]

    for o in z_peers:
        at_recv(o).wait_recv()
        dq_recv(o).wait_recv()
        fk(o, one_of(o), o).wait_recv()
        fv(o, one_of(o), o).wait_recv()
    for o in z_peers:
        kv_send(o).wait_send()
        q_send(o).wait_send()
        at_send(o).wait_send()
        dq_send(o).wait_send()
        fk(o, one_z, z).wait_send()
        fv(o, one_z, z).wait_send()
    for o in p_peers:
        for piece in [z] + z_peers:
            pg_send(o, piece).wait_send()
        red_send(o).wait_send()


def plane_body(
    prefix_keys, prefix_values, round_queries, round_keys, round_values, d_out,
    prefix_agent, prefix_round, round_agent,
):
    pre, own = prefix_keys.shape[0], round_keys.shape[0]
    keys, rows = pre + own, LANES * own
    span, wide = LANES * keys, 4 * rows
    agents = round_agent.reshape(LANES, LANES, own).transpose(1, 0, 2).reshape(LANES, rows)
    vmem = pl.BlockSpec(memory_space=pltpu.VMEM)
    dma = pltpu.SemaphoreType.DMA
    attn, dq, dk, dv = pl.pallas_call(
        functools.partial(plane_kernel, pre, own),
        out_shape=(
            jax.ShapeDtypeStruct(round_queries.shape, BF16),
            jax.ShapeDtypeStruct(round_queries.shape, BF16),
            jax.ShapeDtypeStruct((keys, KVH * DH), BF16),
            jax.ShapeDtypeStruct((keys, KVH * DH), BF16),
        ),
        in_specs=[vmem] * 9,
        out_specs=(vmem,) * 4,
        scratch_shapes=[
            pltpu.VMEM((LANES, 2 * keys, DH), BF16),
            pltpu.VMEM((LANES, 2 * own, 4 * DH), BF16),
            pltpu.VMEM((LANES, LANES, 2 * keys, DH), BF16),
            pltpu.VMEM((LANES, 2 * own, 4 * DH), BF16),
            pltpu.VMEM((LANES, span, DH), BF16),
            pltpu.VMEM((span, rows), F32),
            pltpu.VMEM((2 * DH, wide), BF16),
            pltpu.VMEM((DH, wide), BF16),
            pltpu.VMEM((wide, DH), BF16),
            pltpu.VMEM((wide, DH), BF16),
            pltpu.VMEM((LANES, span, wide), F32),
            pltpu.VMEM((LANES, span, wide), BF16),
            pltpu.VMEM((span, wide), BF16),
            pltpu.VMEM((1, wide), F32),
            pltpu.VMEM((1, wide), F32),
            pltpu.VMEM((DH, wide), F32),
            pltpu.VMEM((LANES, DH, span), BF16),
            pltpu.VMEM((LANES, DH, span), BF16),
            pltpu.VMEM((LANES, own, 4 * DH), BF16),
            pltpu.VMEM((LANES, own, 4 * DH), BF16),
            pltpu.VMEM((LANES, LANES, 2 * keys, DH), BF16),
            pltpu.VMEM((LANES, LANES, 2 * keys, DH), BF16),
            pltpu.VMEM((LANES, 2 * keys, DH), F32),
            pltpu.VMEM((LANES, 2 * keys, DH), BF16),
            dma((LANES,)), dma((LANES,)), dma((LANES,)), dma((LANES,)),
            dma((LANES, LANES)), dma((LANES, LANES)), dma((LANES,)), dma((LANES,)),
            dma((LANES,)), dma((LANES,)), dma((LANES,)), dma((LANES,)),
            dma((LANES,)), dma((LANES,)), dma((LANES,)), dma((LANES,)),
        ],
        compiler_params=pltpu.CompilerParams(
            collective_id=0, has_side_effects=True, vmem_limit_bytes=56 * 1024 * 1024
        ),
    )(
        prefix_keys, prefix_values, round_queries, round_keys, round_values, d_out,
        prefix_agent.reshape(1, -1), prefix_round.reshape(1, -1), agents,
    )
    return attn, dq, dk[pre:], dv[pre:], dk[:pre], dv[:pre]


def solution(mesh):
    placed = (
        P(("group", "seq"), None),
        P(("group", "seq"), None),
        P(("group", "seq"), None),
        P(("group", "seq"), None),
        P(("group", "seq"), None),
        P(("group", "seq"), None),
        P("group"),
        P("group"),
        P("group"),
    )
    planes = mesh.shape["seq"] == KVH * LANES
    return jax.shard_map(
        plane_body if planes else body,
        mesh=mesh,
        in_specs=placed,
        out_specs=(
            P(("group", "seq"), None),
            P(("group", "seq"), None),
            P(("group", "seq"), None),
            P(("group", "seq"), None),
            P(("group", "seq"), None),
            P(("group", "seq"), None),
        ),
        check_vma=False,
    )
```

```python
import functools
import math

import jax
import jax.numpy as jnp
from jax import lax
from jax.experimental import pallas as pl
from jax.experimental.pallas import tpu as pltpu
from jax.sharding import PartitionSpec as P

HQ = 16
KVH = 4
DH = 128
ROUNDS = 16


def to_head_rows(local, devices):
    splits = devices // HQ
    quarter_rows = local.shape[0] // splits
    shaped = local.reshape(splits, quarter_rows, HQ, DH).transpose(2, 0, 1, 3)
    return shaped.reshape(devices, quarter_rows, DH)


def from_head_rows(received, devices):
    splits = devices // HQ
    quarter_rows = received.shape[1]
    shaped = received.reshape(HQ, splits, quarter_rows, DH).transpose(1, 2, 0, 3)
    return shaped.reshape(splits * quarter_rows, HQ * DH)


def spread_heads(local, devices):
    local_keys = local.shape[0]
    shaped = local.reshape(local_keys, KVH, DH).transpose(1, 0, 2)
    shaped = jnp.broadcast_to(shaped[:, None], (KVH, devices // KVH, local_keys, DH))
    return shaped.reshape(devices, local_keys, DH)


def sum_groups(received, devices):
    local_keys = received.shape[1]
    summed = received.reshape(KVH, devices // KVH, local_keys, DH).sum(1)
    return summed.transpose(1, 0, 2).reshape(local_keys, KVH * DH)


def body(
    prefix_keys,
    prefix_values,
    round_queries,
    round_keys,
    round_values,
    d_out,
    prefix_agent,
    prefix_round,
    round_agent,
):
    devices = lax.axis_size("seq")
    device_index = lax.axis_index("seq")
    splits = devices // HQ
    own_rows = round_queries.shape[0]
    quarter_rows = own_rows // splits
    pre_rows = prefix_keys.shape[0]
    local_keys = pre_rows + own_rows
    score_scale = DH ** (-0.5)
    own_block = device_index % splits
    keys_local = jnp.concatenate([prefix_keys, round_keys], 0)
    values_local = jnp.concatenate([prefix_values, round_values], 0)
    query_head, grad_head = (
        lax.all_to_all(
            to_head_rows(round_queries, devices), "seq", split_axis=0, concat_axis=0, tiled=True
        ),
        lax.all_to_all(
            to_head_rows(d_out, devices), "seq", split_axis=0, concat_axis=0, tiled=True
        ),
    )
    query_head = query_head.reshape(devices * quarter_rows, DH)
    grad_head = grad_head.reshape(devices * quarter_rows, DH)
    head_rows = devices * quarter_rows
    key_head, value_head = (
        lax.all_to_all(
            spread_heads(keys_local, devices), "seq", split_axis=0, concat_axis=0, tiled=True
        ),
        lax.all_to_all(
            spread_heads(values_local, devices), "seq", split_axis=0, concat_axis=0, tiled=True
        ),
    )
    source = jnp.arange(devices, dtype=jnp.int32)
    query_pos = (
        source[:, None] * own_rows
        + own_block * quarter_rows
        + jnp.arange(quarter_rows, dtype=jnp.int32)[None, :]
    ).reshape(-1)
    query_agent = round_agent[query_pos]
    key_slot = jnp.arange(local_keys, dtype=jnp.int32)
    pre_index = source[:, None] * pre_rows + jnp.minimum(key_slot, pre_rows - 1)[None, :]
    round_index = source[:, None] * own_rows + jnp.maximum(key_slot - pre_rows, 0)[None, :]
    key_agent = prefix_agent[pre_index]
    key_public = prefix_round[pre_index] < ROUNDS - 2
    key_prefix = jnp.broadcast_to((key_slot < pre_rows)[None, :], (devices, local_keys))
    block_shards = math.gcd(devices, 16)
    blocks = devices // block_shards
    block_keys = block_shards * local_keys
    key_blocks = key_head.reshape(blocks, block_keys, DH)
    value_blocks = value_head.reshape(blocks, block_keys, DH)
    key_info = (
        key_agent.reshape(blocks, block_keys),
        key_public.reshape(blocks, block_keys),
        key_prefix.reshape(blocks, block_keys),
        round_index.reshape(blocks, block_keys),
    )

    def block_scores(key_blk, info):
        agent_b, public_b, prefix_b, order_b = info
        visible = jnp.where(
            prefix_b[None, :],
            public_b[None, :] | (agent_b[None, :] == query_agent[:, None]),
            order_b[None, :] <= query_pos[:, None],
        )
        raw = (
            jnp.einsum("qd,kd->qk", query_head, key_blk, preferred_element_type=jnp.float32)
            * score_scale
        )
        return jnp.where(visible, raw, -jnp.inf)

    def stat_step(carry, blk):
        top, total = carry
        masked = block_scores(blk[0], blk[1])
        new_top = jnp.maximum(top, jnp.max(masked, 1, keepdims=True))
        total = total * jnp.exp(top - new_top) + jnp.sum(
            jnp.exp(masked - new_top), 1, keepdims=True
        )
        return ((new_top, total), None)

    start_stats = (
        jnp.full((head_rows, 1), -1e30, jnp.float32),
        jnp.zeros((head_rows, 1), jnp.float32),
    )
    (top_score, total_exp), _ = lax.scan(stat_step, start_stats, (key_blocks, key_info))
    log_total = top_score + jnp.log(total_exp)

    def out_step(acc, blk):
        masked = block_scores(blk[0], blk[2])
        probs_low = jnp.exp(masked - log_total).astype(jnp.bfloat16)
        return (acc + jnp.dot(probs_low, blk[1], preferred_element_type=jnp.float32), None)

    out_acc, _ = lax.scan(
        out_step, jnp.zeros((head_rows, DH), jnp.float32), (key_blocks, value_blocks, key_info)
    )
    attended = out_acc.astype(jnp.bfloat16)
    attn_rows = lax.all_to_all(
        attended.reshape(devices, quarter_rows, DH), "seq", split_axis=0, concat_axis=0, tiled=True
    )
    attn_out = from_head_rows(attn_rows, devices)
    delta = jnp.sum(grad_head.astype(jnp.float32) * attended.astype(jnp.float32), 1, keepdims=True)

    def back_step(acc, blk):
        key_blk, value_blk, info = blk
        masked = block_scores(key_blk, info)
        probs = jnp.exp(masked - log_total)
        grad_probs = jnp.einsum(
            "qd,kd->qk", grad_head, value_blk, preferred_element_type=jnp.float32
        )
        grad_scores = (probs * (grad_probs - delta) * score_scale).astype(jnp.bfloat16)
        acc = acc + jnp.dot(grad_scores, key_blk, preferred_element_type=jnp.float32)
        key_part = jnp.einsum(
            "qk,qd->kd", grad_scores, query_head, preferred_element_type=jnp.float32
        )
        value_part = jnp.einsum(
            "qk,qd->kd", probs.astype(jnp.bfloat16), grad_head, preferred_element_type=jnp.float32
        )
        return (acc, (key_part, value_part))

    start_grad = jnp.zeros((head_rows, DH), jnp.float32)
    query_acc, parts = lax.scan(
        lambda acc, blk: back_step(acc, blk), start_grad, (key_blocks, value_blocks, key_info)
    )
    key_part = parts[0].reshape(devices, local_keys, DH)
    value_part = parts[1].reshape(devices, local_keys, DH)
    key_sum, value_sum = (
        lax.all_to_all(key_part, "seq", split_axis=0, concat_axis=0, tiled=True),
        lax.all_to_all(value_part, "seq", split_axis=0, concat_axis=0, tiled=True),
    )
    grad_keys = sum_groups(key_sum, devices)
    grad_values = sum_groups(value_sum, devices)
    grad_query = query_acc.astype(jnp.bfloat16)
    query_rows = lax.all_to_all(
        grad_query.reshape(devices, quarter_rows, DH),
        "seq",
        split_axis=0,
        concat_axis=0,
        tiled=True,
    )
    d_round_queries = from_head_rows(query_rows, devices)
    keys_low = grad_keys.astype(jnp.bfloat16)
    values_low = grad_values.astype(jnp.bfloat16)
    return (
        attn_out,
        d_round_queries,
        keys_low[pre_rows:],
        values_low[pre_rows:],
        keys_low[:pre_rows],
        values_low[:pre_rows],
    )


MESH = pl.DeviceIdType.MESH
LANES = 4
BIG = 32768.0
F32 = jnp.float32
BF16 = jnp.bfloat16


def mm(a, b):
    return jnp.dot(a, b, preferred_element_type=F32)


def plane_kernel(
    pre, own,
    pk_ref, pv_ref, q_ref, rk_ref, rv_ref, do_ref, pa_ref, pr_ref, ra_ref,
    attn_ref, dq_ref, dk_ref, dv_ref,
    kv_stage, q_stage, kv_buf, q_buf, kext, tri, qt, dot_t, qs, dos,
    s_buf, p_buf, ds_buf, mx_ref, l_ref, acc_t, kt_buf, vt_buf,
    att_stage, dq_stage, red_stage, red_buf, own_part, fin_stage,
    kvz_s, kvz_r, qz_s, qz_r, pg_s, pg_r, red_s, red_r,
    at_s, at_r, dqs_s, dqs_r, fin_s, fin_r,
):
    keys = pre + own
    rows = LANES * own
    span = LANES * keys
    me = lax.axis_index("seq")
    z = me // LANES
    p = me % LANES
    seq = lambda zz, pp: {"seq": zz * LANES + pp}
    z_peers = [(z + k) % LANES for k in (2, 3, 1)]
    pair = p + 1 - 2 * (p % 2)
    far = (p + 2) % LANES
    cross = pair + 2 - 4 * (pair // 2)
    p_peers = [cross, far, pair]
    scale = DH ** (-0.5)
    to_two = scale * math.log2(math.e)

    def rcopy(src, dst, ss, rs, zz, pp):
        return pltpu.make_async_remote_copy(
            src_ref=src, dst_ref=dst, send_sem=ss, recv_sem=rs,
            device_id=seq(zz, pp), device_id_type=MESH,
        )

    barrier = pltpu.get_barrier_semaphore()
    for o in z_peers:
        pl.semaphore_signal(barrier, inc=1, device_id=seq(o, p), device_id_type=MESH)
    for o in p_peers:
        pl.semaphore_signal(barrier, inc=1, device_id=seq(z, o), device_id_type=MESH)

    for g in range(KVH):
        cols = slice(g * DH, (g + 1) * DH)
        kv_stage[g, 0:pre, :] = pk_ref[:, cols]
        kv_stage[g, pre:keys, :] = rk_ref[:, cols]
        kv_stage[g, keys:keys + pre, :] = pv_ref[:, cols]
        kv_stage[g, keys + pre:2 * keys, :] = rv_ref[:, cols]
        wide = slice(g * 4 * DH, (g + 1) * 4 * DH)
        q_stage[g, 0:own, :] = q_ref[:, wide]
        q_stage[g, own:2 * own, :] = do_ref[:, wide]
    pl.semaphore_wait(barrier, 6)

    def half(i, n):
        return pl.ds(i * n, n)

    def kv_copy(i, o, at, slot):
        return rcopy(
            kv_stage.at[o, half(i, keys)], kv_buf.at[p, at, half(i, keys)],
            kvz_s.at[i, o], kvz_r.at[i, slot], o, p,
        )

    def q_copy(i, o, slot):
        return rcopy(
            q_stage.at[o, half(i, own)], q_buf.at[slot, half(i, own)],
            qz_s.at[i, o], qz_r.at[i, slot], o, p,
        )

    def pg_copy(i, chunk, piece, o, slot):
        return rcopy(
            kv_buf.at[chunk, piece, half(i, keys)], kv_buf.at[chunk, piece, half(i, keys)],
            pg_s.at[i, slot, piece], pg_r.at[i, chunk, piece], z, o,
        )

    pieces = [z] + z_peers

    def pg_mine(i, piece):
        pg_copy(i, p, piece, far, 0).start()
        pg_copy(i, p, piece, pair, 1).start()

    def pg_pass(i, piece):
        pg_copy(i, far, piece, pair, 2).wait_recv()
        pg_copy(i, far, piece, pair, 2).start()

    def pg_wait(i, chunk):
        for piece in pieces:
            pg_copy(i, chunk, piece, pair, 2).wait_recv()

    for i in range(2):
        for o in z_peers:
            kv_copy(i, o, z, z).start()
        for o in z_peers:
            q_copy(i, o, z).start()
    kv_buf[p, z] = kv_stage[z]
    q_buf[z] = q_stage[z]
    pg_mine(0, z)

    lane = lax.broadcasted_iota(jnp.int32, (own, DH), 1) - 16
    sub = lax.broadcasted_iota(jnp.int32, (DH, pre), 0)

    def ext_step(b, carry):
        at = pl.ds(pl.multiple_of(b * pre, pre), pre)
        c = b % LANES
        zz = b // LANES
        base = zz * keys
        off = (pr_ref[:, at] >= ROUNDS - 2) & (pa_ref[:, at] != sub) & (sub < 8)
        kext[c, pl.ds(pl.multiple_of(base, 64), pre), :] = (
            jnp.where(off, 1.0, 0.0).astype(F32).T.astype(BF16)
        )
        late = (lane >= 0) & (lane < b)
        kext[c, pl.ds(pl.multiple_of(base + pre, 64), own), :] = (
            jnp.where(late, 1.0, 0.0).astype(F32).astype(BF16)
        )
        return carry

    lax.fori_loop(0, LANES * LANES, ext_step, 0)
    sub_q = lax.broadcasted_iota(jnp.int32, (DH, rows), 0)
    block_q = (lax.broadcasted_iota(jnp.int32, (DH, rows), 1) // own) * LANES + p
    ext_q = jnp.where(
        ((sub_q < 8) & (sub_q == ra_ref[pl.ds(p, 1), :])) | (sub_q - 16 == block_q), -BIG, 0.0
    ).astype(F32).astype(BF16)
    for h in range(4):
        qt[DH:2 * DH, h * rows:(h + 1) * rows] = ext_q
    row_k = lax.broadcasted_iota(jnp.int32, (span, rows), 0)
    row_q = lax.broadcasted_iota(jnp.int32, (span, rows), 1)
    tri[...] = jnp.where(
        (row_k // keys == row_q // own) & (row_k % keys >= pre)
        & (row_k % keys - pre > row_q % own),
        -BIG, 0.0,
    ).astype(F32)
    mx_ref[...] = jnp.full(mx_ref.shape, -3.0e38, F32)

    for n in range(LANES):
        if n > 0:
            kv_copy(0, pieces[n], pieces[n], pieces[n]).wait_recv()
            pg_mine(0, pieces[n])
            pg_pass(0, pieces[n - 1])
    pg_pass(0, pieces[3])
    pg_mine(1, z)
    for o in z_peers:
        q_copy(0, o, o).wait_recv()
    for h in range(4):
        cols = slice(h * DH, (h + 1) * DH)
        qh = q_buf[:, 0:own, cols].reshape(rows, DH)
        qs[h * rows:(h + 1) * rows, :] = qh
        qt[0:DH, h * rows:(h + 1) * rows] = qh.T

    def head_at(h):
        return pl.ds(pl.multiple_of(h * rows, rows), rows)

    def score_chunk(c, diagonal):
        kc = kv_buf[c, :, 0:keys, :].reshape(span, DH)
        kt_buf[c] = kc.T

        def step(h, carry):
            full = jnp.concatenate(
                [kv_buf[c, :, 0:keys, :].reshape(span, DH), kext[c]], 1
            )
            s = mm(full, qt[:, head_at(h)])
            if diagonal:
                s = s + tri[...]
            s_buf[c, :, head_at(h)] = s
            mx_ref[:, head_at(h)] = jnp.maximum(
                mx_ref[:, head_at(h)], jnp.max(s, 0, keepdims=True)
            )
            return carry

        lax.fori_loop(0, 4, step, 0)

    def turn_values(c):
        vt_buf[c] = kv_buf[c, :, keys:2 * keys, :].reshape(span, DH).T

    score_chunk(p, True)
    pg_wait(0, pair)
    score_chunk(pair, False)
    for o in z_peers:
        kv_copy(1, o, o, o).wait_recv()
        pg_mine(1, o)
    turn_values(p)
    score_chunk(far, False)
    pg_wait(0, cross)
    for piece in pieces:
        pg_pass(1, piece)
    score_chunk(cross, False)
    turn_values(far)
    pg_wait(1, pair)
    turn_values(pair)
    pg_wait(1, cross)
    turn_values(cross)

    def exp_step(h, carry):
        at = head_at(h)
        top = mx_ref[:, at] * to_two
        total = jnp.zeros((1, rows), F32)
        acc = jnp.zeros((DH, rows), F32)
        for c in range(LANES):
            pu = jnp.exp2(s_buf[c, :, at] * to_two - top)
            total = total + jnp.sum(pu, 0, keepdims=True)
            low = pu.astype(BF16)
            p_buf[c, :, at] = low
            acc = acc + mm(vt_buf[c], low)
        inv = 1.0 / total
        l_ref[:, at] = inv
        acc_t[:, at] = (acc * inv).astype(BF16).astype(F32)
        return carry

    lax.fori_loop(0, 4, exp_step, 0)
    for h in range(4):
        cols = slice(h * DH, (h + 1) * DH)
        at = slice(h * rows, (h + 1) * rows)
        att_stage[:, :, cols] = acc_t[:, at].T.astype(BF16).reshape(LANES, own, DH)
    wide_z = pl.ds(pl.multiple_of(z * 4 * DH, 4 * DH), 4 * DH)
    one_z = pl.ds(pl.multiple_of(z * DH, DH), DH)

    def at_send(o):
        return rcopy(att_stage.at[o], attn_ref.at[:, wide_z], at_s.at[o], at_r.at[z], o, p)

    def wide_of(o):
        return pl.ds(pl.multiple_of(o * 4 * DH, 4 * DH), 4 * DH)

    def one_of(o):
        return pl.ds(pl.multiple_of(o * DH, DH), DH)

    def at_recv(o):
        return rcopy(att_stage.at[o], attn_ref.at[:, wide_of(o)], at_s.at[o], at_r.at[o], o, p)

    for o in z_peers:
        at_send(o).start()
    attn_ref[:, wide_z] = att_stage[z]
    for o in z_peers:
        q_copy(1, o, o).wait_recv()
    for h in range(4):
        cols = slice(h * DH, (h + 1) * DH)
        at = slice(h * rows, (h + 1) * rows)
        dh = q_buf[:, own:2 * own, cols].reshape(rows, DH).astype(F32).T
        dot_t[:, at] = dh.astype(BF16)
        mx_ref[:, at] = jnp.sum(acc_t[:, at] * dh, 0, keepdims=True)
        dos[at, :] = (dh * l_ref[:, at]).T.astype(BF16)
    acc_t[...] = jnp.zeros(acc_t.shape, F32)

    def red_copy(i, slot):
        return rcopy(
            red_stage.at[i, slot], red_buf.at[i, slot],
            red_s.at[i, slot], red_r.at[i, slot], z, far if slot == 1 else pair,
        )

    def reduce_sends(i, left, right):
        def part(c):
            return mm(left[c], right[...]).reshape(LANES, keys, DH)

        red_stage[i, 0] = part(cross).astype(BF16)
        red_copy(i, 0).start()
        red_stage[i, 2] = part(pair).astype(BF16)
        red_copy(i, 2).start()
        ours = part(far)
        red_copy(i, 0).wait_recv()
        red_stage[i, 1] = (ours + red_buf[i, 0].astype(F32)).astype(BF16)
        red_copy(i, 1).start()
        own_part[i] = part(p)

    def fin_copy(i, o, at, slot):
        return rcopy(
            fin_stage.at[i, o], (dk_ref, dv_ref)[i].at[:, at],
            fin_s.at[i, o], fin_r.at[i, slot], o, p,
        )

    def finish(i):
        red_copy(i, 2).wait_recv()
        red_copy(i, 1).wait_recv()
        fin_stage[i] = (
            own_part[i] + red_buf[i, 1].astype(F32) + red_buf[i, 2].astype(F32)
        ).astype(BF16)
        for o in z_peers:
            fin_copy(i, o, one_z, z).start()
        (dk_ref, dv_ref)[i][:, one_z] = fin_stage[i, z]

    def grad_chunk(c):
        def step(h, carry):
            at = head_at(h)
            vc = kv_buf[c, :, keys:2 * keys, :].reshape(span, DH)
            dp = mm(vc, dot_t[:, at])
            pu = p_buf[c, :, at].astype(F32)
            ds = (pu * ((dp - mx_ref[:, at]) * (l_ref[:, at] * scale))).astype(BF16)
            ds_buf[c, :, at] = ds
            acc_t[:, at] += mm(kt_buf[c], ds)
            return carry

        lax.fori_loop(0, 4, step, 0)

    reduce_sends(1, p_buf, dos)
    grad_chunk(cross)
    grad_chunk(far)
    finish(1)
    grad_chunk(pair)
    grad_chunk(p)
    for h in range(4):
        cols = slice(h * DH, (h + 1) * DH)
        at = slice(h * rows, (h + 1) * rows)
        dq_stage[:, :, cols] = acc_t[:, at].T.astype(BF16).reshape(LANES, own, DH)

    def dq_send(o):
        return rcopy(dq_stage.at[o], dq_ref.at[:, wide_z], dqs_s.at[o], dqs_r.at[z], o, p)

    def dq_recv(o):
        return rcopy(dq_stage.at[o], dq_ref.at[:, wide_of(o)], dqs_s.at[o], dqs_r.at[o], o, p)

    for o in z_peers:
        dq_send(o).start()
    dq_ref[:, wide_z] = dq_stage[z]

    reduce_sends(0, ds_buf, qs)
    finish(0)

    for o in z_peers:
        at_recv(o).wait_recv()
        dq_recv(o).wait_recv()
        fin_copy(0, o, one_of(o), o).wait_recv()
        fin_copy(1, o, one_of(o), o).wait_recv()
    for o in z_peers:
        at_send(o).wait_send()
        dq_send(o).wait_send()
        for i in range(2):
            kv_copy(i, o, z, z).wait_send()
            q_copy(i, o, z).wait_send()
            fin_copy(i, o, one_z, z).wait_send()
    for i in range(2):
        for slot in range(3):
            red_copy(i, slot).wait_send()
        for piece in pieces:
            pg_copy(i, p, piece, far, 0).wait_send()
            pg_copy(i, p, piece, pair, 1).wait_send()
            pg_copy(i, far, piece, pair, 2).wait_send()


def place_kernel(pre, attn, dq, dk, dv, o_attn, o_dq, o_rk, o_rv, o_pk, o_pv, sems):
    own = dk.shape[0] - pre
    moves = [
        (attn, o_attn), (dq, o_dq),
        (dk.at[pl.ds(pre, own)], o_rk), (dv.at[pl.ds(pre, own)], o_rv),
        (dk.at[pl.ds(0, pre)], o_pk), (dv.at[pl.ds(0, pre)], o_pv),
    ]
    copies = [pltpu.make_async_copy(a, b, sems.at[n]) for n, (a, b) in enumerate(moves)]
    for copy in copies:
        copy.start()
    for copy in copies:
        copy.wait()


def plane_body(
    prefix_keys, prefix_values, round_queries, round_keys, round_values, d_out,
    prefix_agent, prefix_round, round_agent,
):
    pre, own = prefix_keys.shape[0], round_keys.shape[0]
    keys, rows = pre + own, LANES * own
    span, wide = LANES * keys, 4 * rows
    agents = round_agent.reshape(LANES, LANES, own).transpose(1, 0, 2).reshape(LANES, rows)
    vmem = pl.BlockSpec(memory_space=pltpu.VMEM)
    dma = pltpu.SemaphoreType.DMA
    attn, dq, dk, dv = pl.pallas_call(
        functools.partial(plane_kernel, pre, own),
        out_shape=(
            jax.ShapeDtypeStruct(round_queries.shape, BF16),
            jax.ShapeDtypeStruct(round_queries.shape, BF16),
            jax.ShapeDtypeStruct((keys, KVH * DH), BF16),
            jax.ShapeDtypeStruct((keys, KVH * DH), BF16),
        ),
        in_specs=[vmem] * 9,
        out_specs=(vmem,) * 4,
        scratch_shapes=[
            pltpu.VMEM((LANES, 2 * keys, DH), BF16),
            pltpu.VMEM((LANES, 2 * own, 4 * DH), BF16),
            pltpu.VMEM((LANES, LANES, 2 * keys, DH), BF16),
            pltpu.VMEM((LANES, 2 * own, 4 * DH), BF16),
            pltpu.VMEM((LANES, span, DH), BF16),
            pltpu.VMEM((span, rows), F32),
            pltpu.VMEM((2 * DH, wide), BF16),
            pltpu.VMEM((DH, wide), BF16),
            pltpu.VMEM((wide, DH), BF16),
            pltpu.VMEM((wide, DH), BF16),
            pltpu.VMEM((LANES, span, wide), F32),
            pltpu.VMEM((LANES, span, wide), BF16),
            pltpu.VMEM((LANES, span, wide), BF16),
            pltpu.VMEM((1, wide), F32),
            pltpu.VMEM((1, wide), F32),
            pltpu.VMEM((DH, wide), F32),
            pltpu.VMEM((LANES, DH, span), BF16),
            pltpu.VMEM((LANES, DH, span), BF16),
            pltpu.VMEM((LANES, own, 4 * DH), BF16),
            pltpu.VMEM((LANES, own, 4 * DH), BF16),
            pltpu.VMEM((2, 3, LANES, keys, DH), BF16),
            pltpu.VMEM((2, 3, LANES, keys, DH), BF16),
            pltpu.VMEM((2, LANES, keys, DH), F32),
            pltpu.VMEM((2, LANES, keys, DH), BF16),
            dma((2, LANES)), dma((2, LANES)), dma((2, LANES)), dma((2, LANES)),
            dma((2, 3, LANES)), dma((2, LANES, LANES)), dma((2, 3)), dma((2, 3)),
            dma((LANES,)), dma((LANES,)), dma((LANES,)), dma((LANES,)),
            dma((2, LANES)), dma((2, LANES)),
        ],
        compiler_params=pltpu.CompilerParams(
            collective_id=0, has_side_effects=True, vmem_limit_bytes=56 * 1024 * 1024
        ),
    )(
        prefix_keys, prefix_values, round_queries, round_keys, round_values, d_out,
        prefix_agent.reshape(1, -1), prefix_round.reshape(1, -1), agents,
    )
    free = pl.BlockSpec(memory_space=pl.ANY)
    low = lambda a: jax.ShapeDtypeStruct(a.shape, BF16)
    return pl.pallas_call(
        functools.partial(place_kernel, pre),
        out_shape=(
            low(round_queries), low(round_queries), low(round_keys), low(round_keys),
            low(prefix_keys), low(prefix_keys),
        ),
        in_specs=[vmem] * 4,
        out_specs=(free,) * 6,
        scratch_shapes=[dma((6,))],
    )(attn, dq, dk, dv)


def solution(mesh):
    placed = (
        P(("group", "seq"), None),
        P(("group", "seq"), None),
        P(("group", "seq"), None),
        P(("group", "seq"), None),
        P(("group", "seq"), None),
        P(("group", "seq"), None),
        P("group"),
        P("group"),
        P("group"),
    )
    planes = mesh.shape["seq"] == KVH * LANES
    return jax.shard_map(
        plane_body if planes else body,
        mesh=mesh,
        in_specs=placed,
        out_specs=(
            P(("group", "seq"), None),
            P(("group", "seq"), None),
            P(("group", "seq"), None),
            P(("group", "seq"), None),
            P(("group", "seq"), None),
            P(("group", "seq"), None),
        ),
        check_vma=False,
    )
```
